256 devices in a mesh: depth: 64 (over z, y_lo, x), tile: 4 (over y_hi, core).
Axes of the slice: x: 4, y: 4 (y_hi: 2, y_lo: 2; y = y_hi * 2 + y_lo), z: 8, core: 2. Of those that a mesh axis runs over, the one named last changes fastest.
Arguments:
- volume: float32 [2, 64, 225, 512], P(None, 'depth', None, 'tile'), may hold values from 0.1 to 5
- kernel: bfloat16 [64, 225, 81, 225], P('depth'), as said below
- measured: float32 [2, 225, 512], P(None, None, 'tile'), may hold values from 0.2 to 5
Outputs:
- updated: float32 [2, 64, 225, 512], P(None, 'depth', None, 'tile')
The draws below stay inside these ranges and needn't reach their ends.
Inputs may be any that keep to these rules, and one draw needn't show every extreme that they name: `kernel`: kernel weights are nonnegative.
All inputs are finite; a program needn't handle non-finite values.
Results may differ from the reference program's by a relative error of at most 0.0015.
Values may be sent and summed in bfloat16 or wider, within the bound.
A program may use at most 128 MiB of HBM per device.

```python
import math
import jax
import jax.numpy as jnp
from jax import lax

PHASES = 225
KSIDE = 9
KOFF = 81
HALF = 4
DEPTHS = 64
FRAMES = 2
COLS = 32
ROWS = 16


def draw_kernel(key, part):
    key_out = jax.random.fold_in(key, 12)
    key_in = jax.random.fold_in(key, 13)
    key_shift = jax.random.fold_in(key, 15)
    key_plane = jax.random.fold_in(key, 16)
    phase_side = max(math.isqrt(PHASES), 1)
    phase_span = max(phase_side - 1, 1)
    phase_ids = jnp.arange(PHASES, dtype=jnp.int32)
    phase_row = phase_ids // phase_side
    phase_col = phase_ids % phase_side
    step_row = phase_row[:, None] - phase_row[None, :]
    step_col = phase_col[:, None] - phase_col[None, :]
    offset_ids = jnp.arange(KOFF, dtype=jnp.int32)
    offset_row = offset_ids // KSIDE - HALF
    offset_col = offset_ids % KSIDE - HALF
    disparity = jax.random.randint(key_shift, (DEPTHS,), -HALF, HALF + 1, dtype=jnp.int32)
    out_scale = jnp.exp(jax.random.uniform(key_out, (PHASES, 1, 1), jnp.float32) * math.log(10.0))
    in_scale = jnp.exp(jax.random.uniform(key_in, (1, 1, PHASES), jnp.float32) * math.log(10.0))

    def one_plane(inputs):
        plane_index, plane_shift = inputs
        plane_key = jax.random.fold_in(key_plane, plane_index)
        key_jitter = jax.random.fold_in(plane_key, 1)
        key_floor = jax.random.fold_in(plane_key, 2)
        key_target = jax.random.fold_in(plane_key, 3)
        center_row = jnp.clip(plane_shift * step_row // phase_span, -HALF, HALF)
        center_col = jnp.clip(plane_shift * step_col // phase_span, -HALF, HALF)
        apart_row = offset_row[None, :, None] - center_row[:, None, :]
        apart_col = offset_col[None, :, None] - center_col[:, None, :]
        distance = (apart_row * apart_row + apart_col * apart_col).astype(jnp.float32)
        bump_part = jnp.exp(-2.5 * distance)
        jitter = jax.random.uniform(key_jitter, (PHASES, KOFF, PHASES), jnp.float32, 0.5, 1.5)
        floor_part = jax.random.uniform(key_floor, (PHASES, KOFF, PHASES), jnp.float32)
        target = jax.random.randint(key_target, (PHASES,), 0, PHASES, dtype=jnp.int32)
        chosen = (phase_ids[None, :] == target[:, None]).astype(jnp.float32)[:, None, :]
        ray_gain = 1.0 + 2.0 * PHASES * chosen
        return (bump_part * jitter * ray_gain + 0.001 * floor_part) * out_scale * in_scale
    weights = lax.map(one_plane, (jnp.arange(DEPTHS, dtype=jnp.int32), disparity))
    return (weights / (DEPTHS * PHASES * 63.0)).astype(jnp.bfloat16)


def shard_levels(own_key, shape, cuts, low, high):
    loudness, own = 1.0, jax.random.fold_in(own_key, 6)
    for dim, shards_of in cuts:
        draws = jnp.exp(jax.random.uniform(jax.random.fold_in(own, dim), (shards_of,), jnp.float32, low / len(cuts), high / len(cuts)))
        loudness = loudness * jnp.repeat(draws, shape[dim] // shards_of).reshape([-1 if axis == dim else 1 for axis in range(len(shape))])
    return loudness


def setup_inputs(seed: int = 0) -> dict:
    streams_of = jax.random.split(jax.random.key(seed), 4)
    volume = jnp.clip(jnp.exp(math.log(5.0) - 3.912023 * jax.random.uniform(streams_of[0], (FRAMES, DEPTHS, PHASES, ROWS * COLS), jnp.float32) ** shard_levels(streams_of[0], (FRAMES, DEPTHS, PHASES, ROWS * COLS), ((1, 64), (3, 4)), -0.2, 0.2)), 0.1, 5.0)
    kernel = draw_kernel(jax.random.fold_in(streams_of[3], 71), 0)
    measured = jnp.clip(jnp.exp(math.log(5.0) - 3.218876 * jax.random.uniform(streams_of[2], (FRAMES, PHASES, ROWS * COLS), jnp.float32) ** shard_levels(streams_of[2], (FRAMES, PHASES, ROWS * COLS), ((2, 4),), -0.2, 0.2)), 0.2, 5.0)
    return {"volume": volume, "kernel": kernel, "measured": measured}


def stacked(grid, sign, axis):
    rows = grid.shape[1] - 2 * HALF
    cols = grid.shape[2] - 2 * HALF
    pieces = []
    for shift_a in range(-HALF, HALF + 1):
        for shift_b in range(-HALF, HALF + 1):
            top = HALF + sign * shift_a
            left = HALF + sign * shift_b
            pieces.append(grid[:, top:top + rows, left:left + cols].reshape(grid.shape[0], rows * cols))
    return jnp.stack(pieces, axis=axis)


def padded(field):
    return jnp.pad(field.reshape(field.shape[0], ROWS, COLS), ((0, 0), (HALF, HALF), (HALF, HALF)))


def reference(volume, kernel, measured):
    vol16 = volume.astype(jnp.bfloat16)

    def forward(total, inputs):
        kern, vol = inputs
        flat = kern.reshape(PHASES, KOFF * PHASES)
        terms = []
        for frame in range(FRAMES):
            spread = stacked(padded(vol[frame]), 1, 0).reshape(KOFF * PHASES, ROWS * COLS)
            terms.append(jnp.dot(flat, spread, preferred_element_type=jnp.float32))
        return total + jnp.stack(terms), None

    start = jnp.zeros((FRAMES, PHASES, ROWS * COLS), jnp.float32)
    projection, _ = lax.scan(forward, start, (kernel, jnp.moveaxis(vol16, 1, 0)))
    ratio = (measured / projection).astype(jnp.bfloat16)
    spreads = [stacked(padded(ratio[frame]), -1, 1).reshape(PHASES * KOFF, ROWS * COLS) for frame in range(FRAMES)]

    def backward(carry, kern):
        flat = kern.reshape(PHASES * KOFF, PHASES)
        norm = jnp.sum(kern, axis=(0, 1), dtype=jnp.float32)
        backs = [jnp.dot(flat.T, spread, preferred_element_type=jnp.float32) for spread in spreads]
        return carry, jnp.stack(backs) / norm[None, :, None]

    _, scaled = lax.scan(backward, jnp.zeros((), jnp.float32), kernel)
    return volume * jnp.moveaxis(scaled, 0, 1)
```

```python
import functools

import jax
import jax.numpy as jnp
from jax import lax
from jax.experimental import pallas as pl
from jax.experimental.pallas import tpu as pltpu
from jax.sharding import PartitionSpec as P

KSIDE = 9
HALF = 4
COLS = 32
FRAMES = 2
MESH = pl.DeviceIdType.MESH


def step(plane, lines, tiles, vol, ker, meas, out, kbuf, vbuf, mbuf, vx, rx, mt, acc,
         nrm, psend, precv, zsend, zrecv, ksem, lsem, hs, hr, ps, pr, zs, zr, gs, gr):
    phases = ker.shape[2]
    cells = vol.shape[-1]
    rows = FRAMES * cells
    block = rows // plane
    d = lax.axis_index("depth")
    t = lax.axis_index("tile")
    z = d // plane
    k = d % plane
    first = t == 0
    last = t == tiles - 1

    load_vol = pltpu.make_async_copy(vol, vbuf, lsem.at[0])
    load_meas = pltpu.make_async_copy(meas, mbuf, lsem.at[1])
    load_vol.start()
    load_meas.start()

    def load_kernel(b):
        return pltpu.make_async_copy(ker.at[:, b], kbuf.at[b], ksem.at[b])

    for b in range(KSIDE):
        load_kernel(b).start()

    barrier = pltpu.get_barrier_semaphore()
    for j in range(1, plane):
        pl.semaphore_signal(barrier, inc=1, device_id=(z * plane + (k + j) % plane, t), device_id_type=MESH)
    for j in range(1, lines):
        pl.semaphore_signal(barrier, inc=1, device_id=(((z + j) % lines) * plane + k, t), device_id_type=MESH)

    @pl.when(t < tiles - 1)
    def _():
        for j in range(plane):
            pl.semaphore_signal(barrier, inc=1, device_id=(z * plane + (k + j) % plane, t + 1), device_id_type=MESH)

    @pl.when(t > 0)
    def _():
        for j in range(plane):
            pl.semaphore_signal(barrier, inc=1, device_id=(z * plane + (k + j) % plane, t - 1), device_id_type=MESH)

    @pl.when(first)
    def _():
        vx[:, 0:cells, :] = jnp.zeros((FRAMES, cells, phases), jnp.bfloat16)
        rx[:, 0:cells, :] = jnp.zeros((FRAMES, cells, phases), jnp.bfloat16)

    @pl.when(last)
    def _():
        vx[:, 2 * cells:, :] = jnp.zeros((FRAMES, cells, phases), jnp.bfloat16)
        rx[:, 2 * cells:, :] = jnp.zeros((FRAMES, cells, phases), jnp.bfloat16)

    load_vol.wait()
    for f in range(FRAMES):
        vx[f, cells:2 * cells, :] = vbuf[f, :, 0, :].T.astype(jnp.bfloat16)

    sides = jnp.where(t > 0, 1, 0) + jnp.where(t < tiles - 1, 1, 0)
    pl.semaphore_wait(barrier, plane - 1 + lines - 1 + plane * sides)

    own = vx.at[:, pl.ds(cells, cells), :]
    to_next = pltpu.make_async_remote_copy(
        own, vx.at[:, pl.ds(0, cells), :], hs.at[0], hr.at[0], device_id=(d, t + 1), device_id_type=MESH)
    to_prev = pltpu.make_async_remote_copy(
        own, vx.at[:, pl.ds(2 * cells, cells), :], hs.at[1], hr.at[1], device_id=(d, t - 1), device_id_type=MESH)

    @pl.when(t < tiles - 1)
    def _():
        to_next.start()

    @pl.when(t > 0)
    def _():
        to_prev.start()

    load_meas.wait()
    for f in range(FRAMES):
        mt[f * cells:(f + 1) * cells, :] = mbuf[:, f, :].T

    nrm[...] = jnp.zeros_like(nrm)

    @pl.loop(0, KSIDE)
    def _(b):
        load_kernel(b).wait()
        total = jnp.zeros((1, phases), jnp.float32)
        for a in range(KSIDE):
            total += jnp.sum(kbuf[b, a].astype(jnp.float32), axis=0, keepdims=True)
        nrm[0:1, :] += total

    @pl.when(t > 0)
    def _():
        to_next.wait_recv()

    @pl.when(t < tiles - 1)
    def _():
        to_prev.wait_recv()

    column = lax.broadcasted_iota(jnp.int32, (rows, phases), 0) % COLS

    acc[...] = jnp.zeros_like(acc)

    @pl.loop(0, KSIDE)
    def _(b):
        total = jnp.zeros((rows, phases), jnp.float32)
        for a in range(KSIDE):
            lhs = vx[:, COLS * a:COLS * a + cells, :].reshape(rows, phases)
            total += lax.dot_general(lhs, kbuf[b, a], (((1,), (1,)), ((), ())), preferred_element_type=jnp.float32)
        shift = b - HALF
        moved = column + shift
        keep = (moved >= 0) & (moved < COLS)
        acc[...] += jnp.where(keep, pltpu.roll(total, (rows - shift) % rows, 0), 0.0)

    psend[...] = acc[...].astype(jnp.bfloat16)
    sends = []
    for j in range(1, plane):
        peer = (k + j) % plane
        copy = pltpu.make_async_remote_copy(
            psend.at[pl.ds(pl.multiple_of(peer * block, block), block), :], precv.at[j], ps.at[j], pr.at[j],
            device_id=(z * plane + peer, t), device_id_type=MESH)
        copy.start()
        sends.append(copy)
    mine = pl.ds(pl.multiple_of(k * block, block), block)
    part = acc[mine, :]
    for j in range(1, plane):
        sends[j - 1].wait_recv()
        part += precv[j].astype(jnp.float32)

    zsend[...] = part.astype(jnp.bfloat16)
    for j in range(1, lines):
        peer = (z + j) % lines
        copy = pltpu.make_async_remote_copy(
            zsend, zrecv.at[j], zs.at[j], zr.at[j], device_id=(peer * plane + k, t), device_id_type=MESH)
        copy.start()
        sends.append(copy)
    for j in range(1, lines):
        sends[plane - 1 + j - 1].wait_recv()
        part += zrecv[j].astype(jnp.float32)

    ratio = (mt[mine, :] / part).astype(jnp.bfloat16)
    fk = (k * block) // cells
    rk = (k * block) % cells

    def place(base):
        return rx.at[fk, pl.ds(pl.multiple_of(base + rk, block), block), :]

    rx[fk, pl.ds(pl.multiple_of(cells + rk, block), block), :] = ratio

    def gather(side, j):
        return pltpu.make_async_remote_copy(
            place(cells), place((1 - side) * cells), gs.at[side + 1, j], gr.at[side + 1, j],
            device_id=(z * plane + (k + j) % plane, t + side), device_id_type=MESH)

    for j in range(1, plane):
        gather(0, j).start()

    @pl.when(t < tiles - 1)
    def _():
        for j in range(plane):
            gather(1, j).start()

    @pl.when(t > 0)
    def _():
        for j in range(plane):
            gather(-1, j).start()

    for j in range(1, plane):
        gather(0, j).wait_recv()

    @pl.when(t > 0)
    def _():
        for j in range(plane):
            gather(1, j).wait_recv()

    @pl.when(t < tiles - 1)
    def _():
        for j in range(plane):
            gather(-1, j).wait_recv()

    acc[...] = jnp.zeros_like(acc)

    @pl.loop(0, KSIDE)
    def _(b):
        total = jnp.zeros((rows, phases), jnp.float32)
        for a in range(KSIDE):
            low = 2 * cells - COLS * a
            lhs = rx[:, low:low + cells, :].reshape(rows, phases)
            total += jnp.dot(lhs, kbuf[b, a], preferred_element_type=jnp.float32)
        shift = b - HALF
        moved = column - shift
        keep = (moved >= 0) & (moved < COLS)
        acc[...] += jnp.where(keep, pltpu.roll(total, (rows + shift) % rows, 0), 0.0)

    norm = nrm[0:1, :]
    for f in range(FRAMES):
        scaled = acc[f * cells:(f + 1) * cells, :] / norm
        out[f, :, 0, :] = vbuf[f, :, 0, :] * scaled.T

    for copy in sends:
        copy.wait_send()
    for j in range(1, plane):
        gather(0, j).wait_send()

    @pl.when(t < tiles - 1)
    def _():
        to_next.wait_send()
        for j in range(plane):
            gather(1, j).wait_send()

    @pl.when(t > 0)
    def _():
        to_prev.wait_send()
        for j in range(plane):
            gather(-1, j).wait_send()


def local(depths, tiles, volume, kernel, measured):
    frames, _, phases, cells = volume.shape
    plane = 8 if depths % 8 == 0 else 2
    lines = depths // plane
    rows = frames * cells
    block = rows // plane
    vol = volume.transpose(0, 2, 1, 3)
    ker = kernel.transpose(0, 2, 1, 3).reshape(KSIDE, KSIDE, phases, phases)
    meas = measured.transpose(1, 0, 2)
    bf16, f32 = jnp.bfloat16, jnp.float32
    dma = pltpu.SemaphoreType.DMA
    out = pl.pallas_call(
        functools.partial(step, plane, lines, tiles),
        out_shape=jax.ShapeDtypeStruct((frames, phases, 1, cells), f32),
        in_specs=[pl.BlockSpec(memory_space=pl.ANY)] * 3,
        out_specs=pl.BlockSpec(memory_space=pltpu.VMEM),
        scratch_shapes=[
            pltpu.VMEM((KSIDE, KSIDE, phases, phases), bf16),
            pltpu.VMEM((frames, phases, 1, cells), f32),
            pltpu.VMEM((phases, frames, cells), f32),
            pltpu.VMEM((frames, 3 * cells, phases), bf16),
            pltpu.VMEM((frames, 3 * cells, phases), bf16),
            pltpu.VMEM((rows, phases), f32),
            pltpu.VMEM((rows, phases), f32),
            pltpu.VMEM((8, phases), f32),
            pltpu.VMEM((rows, phases), bf16),
            pltpu.VMEM((plane, block, phases), bf16),
            pltpu.VMEM((block, phases), bf16),
            pltpu.VMEM((lines, block, phases), bf16),
            dma((KSIDE,)), dma((2,)), dma((2,)), dma((2,)),
            dma((plane,)), dma((plane,)), dma((lines,)), dma((lines,)),
            dma((3, plane)), dma((3, plane)),
        ],
        compiler_params=pltpu.CompilerParams(
            collective_id=0, has_side_effects=True),
    )(vol, ker, meas)
    return out.transpose(0, 2, 1, 3)


def solution(mesh):
    in_specs = (P(None, "depth", None, "tile"), P("depth", None, None, None), P(None, None, "tile"))
    out_specs = P(None, "depth", None, "tile")
    return jax.shard_map(
        functools.partial(local, mesh.shape["depth"], mesh.shape["tile"]),
        mesh=mesh, in_specs=in_specs, out_specs=out_specs, check_vma=False)
```

```python
import functools

import jax
import jax.numpy as jnp
from jax import lax
from jax.experimental import pallas as pl
from jax.experimental.pallas import tpu as pltpu
from jax.sharding import PartitionSpec as P

KSIDE = 9
HALF = 4
COLS = 32
FRAMES = 2
MESH = pl.DeviceIdType.MESH


def partial_sums(src, taps, sign, cells, own, transposed):
    height = cells // COLS
    phases = src.shape[-1]
    sums = [None] * height
    for a in range(KSIDE):
        u = sign * (a - HALF)
        if own:
            low, high = max(0, -u), min(height, height - u)
        else:
            low, high = (max(0, height - u), height) if u > 0 else (0, min(height, -u))
        if low >= high:
            continue
        start = cells + COLS * (low + u)
        count = high - low
        lhs = src[:, start:start + COLS * count, :].reshape(FRAMES * COLS * count, phases)
        dims = (((1,), (1 if transposed else 0,)), ((), ()))
        out = lax.dot_general(lhs, taps[a], dims, preferred_element_type=jnp.float32)
        out = out.reshape(FRAMES, count, COLS, phases)
        for i in range(count):
            piece = out[:, i]
            sums[low + i] = piece if sums[low + i] is None else sums[low + i] + piece
    return jnp.stack(sums, axis=1).reshape(FRAMES * cells, phases)


def step(plane, lines, tiles, vol, ker, meas, out, kbuf, vbuf, mbuf, vx, rx, mt, acc, parts,
         nrm, psend, precv, zsend, zrecv, ksem, lsem, hs, hr, ps, pr, zs, zr, gs, gr, round_sem):
    phases = ker.shape[2]
    cells = vol.shape[-1]
    rows = FRAMES * cells
    block = rows // plane
    d = lax.axis_index("depth")
    t = lax.axis_index("tile")
    z = d // plane
    k = d % plane
    first = t == 0
    last = t == tiles - 1

    load_vol = pltpu.make_async_copy(vol, vbuf, lsem.at[0])
    load_meas = pltpu.make_async_copy(meas, mbuf, lsem.at[1])
    load_vol.start()

    def load_kernel(b):
        return pltpu.make_async_copy(ker.at[:, b], kbuf.at[b], ksem.at[b])

    pair = 1 - 2 * (t % 2)
    far = t - pair
    crossing = (far >= 0) & (far < tiles)
    relayed = plane == 8 and lines == 8

    def tell(sem, depth, tile):
        pl.semaphore_signal(sem, inc=1, device_id=(depth, tile), device_id_type=MESH)

    def along(j):
        return ((z + lines + j) % lines) * plane + k

    def flat(j):
        return z * plane + (k + j) % plane

    across = z * plane + (k + plane // 2) % plane
    barrier = pltpu.get_barrier_semaphore()
    if relayed:
        row = z * plane + (k // 4) * 4
        for j in range(1, 4):
            tell(barrier, row + (k + j) % 4, t)
        tell(barrier, across, t)
        for j in (-2, -1, 1, 2):
            tell(barrier, along(j), t)
        near = 8
    else:
        for j in range(1, plane):
            tell(barrier, flat(j), t)
        for j in range(1, lines):
            tell(barrier, along(j), t)
        near = plane + lines - 2
    tell(barrier, d, t + pair)

    @pl.when(crossing)
    def _():
        tell(barrier, d, far)

    @pl.when(first)
    def _():
        vx[:, 0:cells, :] = jnp.zeros((FRAMES, cells, phases), jnp.bfloat16)
        rx[:, 0:cells, :] = jnp.zeros((FRAMES, cells, phases), jnp.bfloat16)

    @pl.when(last)
    def _():
        vx[:, 2 * cells:, :] = jnp.zeros((FRAMES, cells, phases), jnp.bfloat16)
        rx[:, 2 * cells:, :] = jnp.zeros((FRAMES, cells, phases), jnp.bfloat16)

    load_vol.wait()
    for b in range(KSIDE):
        load_kernel(b).start()
    load_meas.start()
    for f in range(FRAMES):
        vx[f, cells:2 * cells, :] = vbuf[f, :, 0, :].T.astype(jnp.bfloat16)

    pl.semaphore_wait(barrier, near + 1 + jnp.where(crossing, 1, 0))

    own = vx.at[:, pl.ds(cells, cells), :]
    to_next = pltpu.make_async_remote_copy(
        own, vx.at[:, pl.ds(0, cells), :], hs.at[0], hr.at[0], device_id=(d, t + 1), device_id_type=MESH)
    to_prev = pltpu.make_async_remote_copy(
        own, vx.at[:, pl.ds(2 * cells, cells), :], hs.at[1], hr.at[1], device_id=(d, t - 1), device_id_type=MESH)

    @pl.when(t < tiles - 1)
    def _():
        to_next.start()

    @pl.when(t > 0)
    def _():
        to_prev.start()

    if relayed:
        tell(round_sem.at[0], along(-2), t)
        tell(round_sem.at[1], along(2), t)
        tell(round_sem.at[2], across, t)

    load_meas.wait()
    for f in range(FRAMES):
        mt[f * cells:(f + 1) * cells, :] = mbuf[:, f, :].T

    @pl.loop(0, KSIDE)
    def _(b):
        load_kernel(b).wait()
        parts[b] = partial_sums(vx, kbuf.at[b], 1, cells, True, True)

    if relayed:
        pl.semaphore_wait(round_sem.at[2], 1)
    @pl.when(crossing)
    def _():
        tell(round_sem.at[3], d, far)

    @pl.when(t > 0)
    def _():
        to_next.wait_recv()

    @pl.when(t < tiles - 1)
    def _():
        to_prev.wait_recv()

    column = lax.broadcasted_iota(jnp.int32, (rows, phases), 0) % COLS

    def shifted(total, shift):
        if shift == 0:
            return total
        moved = column - shift
        return jnp.where((moved >= 0) & (moved < COLS), pltpu.roll(total, shift % rows, 0), 0.0)

    for b in range(KSIDE):
        total = parts[b] + partial_sums(vx, kbuf.at[b], 1, cells, False, True)
        add = shifted(total, HALF - b)
        acc[...] = add if b == 0 else acc[...] + add

    if relayed:
        pl.semaphore_wait(round_sem.at[0], 1)
        pl.semaphore_wait(round_sem.at[1], 1)

    @pl.when(crossing)
    def _():
        pl.semaphore_wait(round_sem.at[3], 1)

    psend[...] = acc[...].astype(jnp.bfloat16)
    sends = []
    for j in range(1, plane):
        peer = (k + j) % plane
        copy = pltpu.make_async_remote_copy(
            psend.at[pl.ds(pl.multiple_of(peer * block, block), block), :], precv.at[j], ps.at[j], pr.at[j],
            device_id=(z * plane + peer, t), device_id_type=MESH)
        copy.start()
        sends.append(copy)
    nrm[...] = jnp.zeros_like(nrm)

    @pl.loop(0, KSIDE)
    def _(b):
        total = jnp.zeros((1, phases), jnp.float32)
        for a in range(KSIDE):
            total += jnp.sum(kbuf[b, a].astype(jnp.float32), axis=0, keepdims=True)
        nrm[0:1, :] += total

    mine = pl.ds(pl.multiple_of(k * block, block), block)
    part = acc[mine, :]
    for j in range(1, plane):
        sends[j - 1].wait_recv()
        part += precv[j].astype(jnp.float32)

    zsend[...] = part.astype(jnp.bfloat16)
    for j in range(1, lines):
        peer = (z + j) % lines
        copy = pltpu.make_async_remote_copy(
            zsend, zrecv.at[j], zs.at[j], zr.at[j], device_id=(peer * plane + k, t), device_id_type=MESH)
        copy.start()
        sends.append(copy)
    for j in range(1, lines):
        sends[plane - 1 + j - 1].wait_recv()
        part += zrecv[j].astype(jnp.float32)

    ratio = (mt[mine, :] / part).astype(jnp.bfloat16)
    fk = (k * block) // cells
    rk = (k * block) % cells

    def place(base, who):
        f = (who * block) // cells
        r = (who * block) % cells
        return rx.at[f, pl.ds(pl.multiple_of(base + r, block), block), :]

    rx[fk, pl.ds(pl.multiple_of(cells + rk, block), block), :] = ratio

    def gather(j):
        return pltpu.make_async_remote_copy(
            place(cells, k), place(cells, k), gs.at[0, j], gr.at[0, j],
            device_id=(z * plane + (k + j) % plane, t), device_id_type=MESH)

    def cross(j):
        return pltpu.make_async_remote_copy(
            place(cells, k), place((1 + pair) * cells, k), gs.at[1, j], gr.at[1, j],
            device_id=(z * plane + (k + j) % plane, far), device_id_type=MESH)

    def relay(j):
        who = (k + plane - j) % plane
        return pltpu.make_async_remote_copy(
            place(cells, who), place((1 - pair) * cells, who), gs.at[2, j], gr.at[2, j],
            device_id=(d, t + pair), device_id_type=MESH)

    for j in range(1, plane):
        gather(j).start()

    @pl.when(crossing)
    def _():
        for j in range(plane):
            cross(j).start()

    relay(0).start()
    for j in range(1, plane):
        gather(j).wait_recv()
        relay(j).start()

    @pl.loop(0, KSIDE)
    def _(b):
        parts[b] = partial_sums(rx, kbuf.at[b], -1, cells, True, False)

    for j in range(plane):
        relay(j).wait_recv()

    @pl.when(crossing)
    def _():
        for j in range(plane):
            cross(j).wait_recv()

    for b in range(KSIDE):
        total = parts[b] + partial_sums(rx, kbuf.at[b], -1, cells, False, False)
        add = shifted(total, b - HALF)
        acc[...] = add if b == 0 else acc[...] + add

    norm = nrm[0:1, :]
    for f in range(FRAMES):
        scaled = acc[f * cells:(f + 1) * cells, :] / norm
        out[f, :, 0, :] = vbuf[f, :, 0, :] * scaled.T

    for copy in sends:
        copy.wait_send()
    for j in range(1, plane):
        gather(j).wait_send()
    for j in range(plane):
        relay(j).wait_send()

    @pl.when(crossing)
    def _():
        for j in range(plane):
            cross(j).wait_send()

    @pl.when(t < tiles - 1)
    def _():
        to_next.wait_send()

    @pl.when(t > 0)
    def _():
        to_prev.wait_send()


def local(depths, tiles, volume, kernel, measured):
    frames, _, phases, cells = volume.shape
    plane = 8 if depths % 8 == 0 else 2
    lines = depths // plane
    rows = frames * cells
    block = rows // plane
    vol = volume.transpose(0, 2, 1, 3)
    ker = kernel.transpose(0, 2, 1, 3).reshape(KSIDE, KSIDE, phases, phases)
    meas = measured.transpose(1, 0, 2)
    bf16, f32 = jnp.bfloat16, jnp.float32
    dma = pltpu.SemaphoreType.DMA
    out = pl.pallas_call(
        functools.partial(step, plane, lines, tiles),
        out_shape=jax.ShapeDtypeStruct((frames, phases, 1, cells), f32),
        in_specs=[pl.BlockSpec(memory_space=pl.ANY)] * 3,
        out_specs=pl.BlockSpec(memory_space=pltpu.VMEM),
        scratch_shapes=[
            pltpu.VMEM((KSIDE, KSIDE, phases, phases), bf16),
            pltpu.VMEM((frames, phases, 1, cells), f32),
            pltpu.VMEM((phases, frames, cells), f32),
            pltpu.VMEM((frames, 3 * cells, phases), bf16),
            pltpu.VMEM((frames, 3 * cells, phases), bf16),
            pltpu.VMEM((rows, phases), f32),
            pltpu.VMEM((rows, phases), f32),
            pltpu.VMEM((KSIDE, rows, phases), f32),
            pltpu.VMEM((8, phases), f32),
            pltpu.VMEM((rows, phases), bf16),
            pltpu.VMEM((plane, block, phases), bf16),
            pltpu.VMEM((block, phases), bf16),
            pltpu.VMEM((lines, block, phases), bf16),
            dma((KSIDE,)), dma((2,)), dma((2,)), dma((2,)),
            dma((plane,)), dma((plane,)), dma((lines,)), dma((lines,)),
            dma((3, plane)), dma((3, plane)),
            pltpu.SemaphoreType.REGULAR((4,)),
        ],
        compiler_params=pltpu.CompilerParams(
            collective_id=0, has_side_effects=True),
    )(vol, ker, meas)
    return out.transpose(0, 2, 1, 3)


def solution(mesh):
    in_specs = (P(None, "depth", None, "tile"), P("depth", None, None, None), P(None, None, "tile"))
    out_specs = P(None, "depth", None, "tile")
    return jax.shard_map(
        functools.partial(local, mesh.shape["depth"], mesh.shape["tile"]),
        mesh=mesh, in_specs=in_specs, out_specs=out_specs, check_vma=False)
```

```python
import functools

import jax
import jax.numpy as jnp
from jax import lax
from jax.experimental import pallas as pl
from jax.experimental.pallas import tpu as pltpu
from jax.sharding import PartitionSpec as P

KSIDE = 9
HALF = 4
COLS = 32
FRAMES = 2
MESH = pl.DeviceIdType.MESH


def partial_sums(src, taps, sign, cells, own, transposed):
    height = cells // COLS
    phases = src.shape[-1]
    sums = [None] * height
    for a in range(KSIDE):
        u = sign * (a - HALF)
        if own:
            low, high = max(0, -u), min(height, height - u)
        else:
            low, high = (max(0, height - u), height) if u > 0 else (0, min(height, -u))
        if low >= high:
            continue
        start = cells + COLS * (low + u)
        count = high - low
        lhs = src[:, start:start + COLS * count, :].reshape(FRAMES * COLS * count, phases)
        dims = (((1,), (1 if transposed else 0,)), ((), ()))
        out = lax.dot_general(lhs, taps[a], dims, preferred_element_type=jnp.float32)
        out = out.reshape(FRAMES, count, COLS, phases)
        for i in range(count):
            piece = out[:, i]
            sums[low + i] = piece if sums[low + i] is None else sums[low + i] + piece
    return jnp.stack(sums, axis=1).reshape(FRAMES * cells, phases)


def step(plane, lines, tiles, vol, ker, meas, out, kbuf, vbuf, mbuf, vx, rx, mt, acc, parts,
         nrm, psend, precv, zsend, zrecv, ksem, lsem, hs, hr, ps, pr, zs, zr, gs, gr, round_sem):
    phases = ker.shape[2]
    cells = vol.shape[-1]
    rows = FRAMES * cells
    block = rows // plane
    d = lax.axis_index("depth")
    t = lax.axis_index("tile")
    z = d // plane
    k = d % plane
    first = t == 0
    last = t == tiles - 1

    load_vol = pltpu.make_async_copy(vol, vbuf, lsem.at[0])
    load_meas = pltpu.make_async_copy(meas, mbuf, lsem.at[1])
    load_vol.start()

    def load_kernel(b):
        return pltpu.make_async_copy(ker.at[:, b], kbuf.at[b], ksem.at[b])

    pair = 1 - 2 * (t % 2)
    far = t - pair
    crossing = (far >= 0) & (far < tiles)
    relayed = plane == 8 and lines == 8

    def tell(sem, depth, tile):
        pl.semaphore_signal(sem, inc=1, device_id=(depth, tile), device_id_type=MESH)

    def along(j):
        return ((z + lines + j) % lines) * plane + k

    def flat(j):
        return z * plane + (k + j) % plane

    across = z * plane + (k + plane // 2) % plane
    barrier = pltpu.get_barrier_semaphore()
    if relayed:
        row = z * plane + (k // 4) * 4
        for j in range(1, 4):
            tell(barrier, row + (k + j) % 4, t)
        tell(barrier, across, t)
        for j in (-2, -1, 1, 2):
            tell(barrier, along(j), t)
        near = 8
    else:
        for j in range(1, plane):
            tell(barrier, flat(j), t)
        for j in range(1, lines):
            tell(barrier, along(j), t)
        near = plane + lines - 2
    tell(barrier, d, t + pair)

    @pl.when(crossing)
    def _():
        tell(barrier, d, far)

    @pl.when(first)
    def _():
        vx[:, 0:cells, :] = jnp.zeros((FRAMES, cells, phases), jnp.bfloat16)
        rx[:, 0:cells, :] = jnp.zeros((FRAMES, cells, phases), jnp.bfloat16)

    @pl.when(last)
    def _():
        vx[:, 2 * cells:, :] = jnp.zeros((FRAMES, cells, phases), jnp.bfloat16)
        rx[:, 2 * cells:, :] = jnp.zeros((FRAMES, cells, phases), jnp.bfloat16)

    load_vol.wait()
    for b in range(KSIDE):
        load_kernel(b).start()
    load_meas.start()
    for f in range(FRAMES):
        vx[f, cells:2 * cells, :] = vbuf[f, :, 0, :].T.astype(jnp.bfloat16)

    pl.semaphore_wait(barrier, near + 1 + jnp.where(crossing, 1, 0))

    own = vx.at[:, pl.ds(cells, cells), :]
    to_next = pltpu.make_async_remote_copy(
        own, vx.at[:, pl.ds(0, cells), :], hs.at[0], hr.at[0], device_id=(d, t + 1), device_id_type=MESH)
    to_prev = pltpu.make_async_remote_copy(
        own, vx.at[:, pl.ds(2 * cells, cells), :], hs.at[1], hr.at[1], device_id=(d, t - 1), device_id_type=MESH)

    @pl.when(t < tiles - 1)
    def _():
        to_next.start()

    @pl.when(t > 0)
    def _():
        to_prev.start()

    if relayed:
        tell(round_sem.at[0], along(-2), t)
        tell(round_sem.at[1], along(2), t)
        tell(round_sem.at[2], across, t)

    load_meas.wait()
    for f in range(FRAMES):
        mt[f * cells:(f + 1) * cells, :] = mbuf[:, f, :].T

    @pl.loop(0, KSIDE)
    def _(b):
        load_kernel(b).wait()
        parts[b] = partial_sums(vx, kbuf.at[b], 1, cells, True, True)

    if relayed:
        pl.semaphore_wait(round_sem.at[2], 1)
    @pl.when(crossing)
    def _():
        tell(round_sem.at[3], d, far)

    @pl.when(t > 0)
    def _():
        to_next.wait_recv()

    @pl.when(t < tiles - 1)
    def _():
        to_prev.wait_recv()

    column = lax.broadcasted_iota(jnp.int32, (rows, phases), 0) % COLS

    def shifted(total, shift):
        if shift == 0:
            return total
        moved = column - shift
        return jnp.where((moved >= 0) & (moved < COLS), pltpu.roll(total, shift % rows, 0), 0.0)

    for b in range(KSIDE):
        total = parts[b] + partial_sums(vx, kbuf.at[b], 1, cells, False, True)
        add = shifted(total, HALF - b)
        acc[...] = add if b == 0 else acc[...] + add

    if relayed:
        pl.semaphore_wait(round_sem.at[0], 1)
        pl.semaphore_wait(round_sem.at[1], 1)

    @pl.when(crossing)
    def _():
        pl.semaphore_wait(round_sem.at[3], 1)

    psend[...] = acc[...].astype(jnp.bfloat16)
    for j in range(1, plane):
        peer = (k + j) % plane
        pltpu.make_async_remote_copy(
            psend.at[pl.ds(pl.multiple_of(peer * block, block), block), :], precv.at[j], ps, pr,
            device_id=(z * plane + peer, t), device_id_type=MESH).start()

    def landed(ref, sem):
        pltpu.make_async_copy(ref, ref, sem).wait()

    others = pl.ds(1, plane - 1)
    mine = pl.ds(pl.multiple_of(k * block, block), block)
    part = acc[mine, :]
    landed(precv.at[others], pr)
    for j in range(1, plane):
        part += precv[j].astype(jnp.float32)

    zsend[...] = part.astype(jnp.bfloat16)
    for j in range(1, lines):
        pltpu.make_async_remote_copy(
            zsend, zrecv.at[j], zs, zr, device_id=(along(j), t), device_id_type=MESH).start()
    landed(zrecv.at[pl.ds(1, lines - 1)], zr)
    for j in range(1, lines):
        part += zrecv[j].astype(jnp.float32)

    ratio = (mt[mine, :] / part).astype(jnp.bfloat16)
    fk = (k * block) // cells
    rk = (k * block) % cells

    def place(base, who):
        f = (who * block) // cells
        r = (who * block) % cells
        return rx.at[f, pl.ds(pl.multiple_of(base + r, block), block), :]

    rx[fk, pl.ds(pl.multiple_of(cells + rk, block), block), :] = ratio

    for j in range(1, plane):
        pltpu.make_async_remote_copy(
            place(cells, k), place(cells, k), gs.at[0], gr.at[0],
            device_id=(flat(j), t), device_id_type=MESH).start()

    @pl.when(crossing)
    def _():
        for j in range(plane):
            pltpu.make_async_remote_copy(
                place(cells, k), place((1 + pair) * cells, k), gs.at[1], gr.at[1],
                device_id=(flat(j), far), device_id_type=MESH).start()

    ones = jnp.ones((16, phases), jnp.bfloat16)
    nrm[...] = jnp.zeros_like(nrm)

    @pl.loop(0, KSIDE)
    def _(b):
        total = None
        for a in range(KSIDE):
            term = jnp.dot(ones, kbuf[b, a], preferred_element_type=jnp.float32)
            total = term if total is None else total + term
        nrm[...] += total

    relay = pltpu.make_async_remote_copy(
        rx.at[:, pl.ds(cells, cells), :], rx.at[:, pl.ds(pl.multiple_of((1 - pair) * cells, cells), cells), :],
        gs.at[2], gr.at[2], device_id=(d, t + pair), device_id_type=MESH)
    landed(precv.at[others], gr.at[0])
    relay.start()

    @pl.loop(0, KSIDE, unroll=3)
    def _(b):
        parts[b] = partial_sums(rx, kbuf.at[b], -1, cells, True, False)

    relay.wait_recv()

    @pl.when(crossing)
    def _():
        landed(rx.at[:, pl.ds(0, cells), :], gr.at[1])

    for b in range(KSIDE):
        total = parts[b] + partial_sums(rx, kbuf.at[b], -1, cells, False, False)
        add = shifted(total, b - HALF)
        acc[...] = add if b == 0 else acc[...] + add

    norm = nrm[0:1, :]
    for f in range(FRAMES):
        scaled = acc[f * cells:(f + 1) * cells, :] / norm
        out[f, :, 0, :] = vbuf[f, :, 0, :] * scaled.T

    landed(precv.at[others], ps)
    landed(zrecv.at[pl.ds(1, lines - 1)], zs)
    landed(precv.at[others], gs.at[0])
    relay.wait_send()

    @pl.when(crossing)
    def _():
        landed(rx.at[:, pl.ds(0, cells), :], gs.at[1])

    @pl.when(t < tiles - 1)
    def _():
        to_next.wait_send()

    @pl.when(t > 0)
    def _():
        to_prev.wait_send()


def local(depths, tiles, volume, kernel, measured):
    frames, _, phases, cells = volume.shape
    plane = 8 if depths % 8 == 0 else 2
    lines = depths // plane
    rows = frames * cells
    block = rows // plane
    vol = volume.transpose(0, 2, 1, 3)
    ker = kernel.transpose(0, 2, 1, 3).reshape(KSIDE, KSIDE, phases, phases)
    meas = measured.transpose(1, 0, 2)
    bf16, f32 = jnp.bfloat16, jnp.float32
    dma = pltpu.SemaphoreType.DMA
    out = pl.pallas_call(
        functools.partial(step, plane, lines, tiles),
        out_shape=jax.ShapeDtypeStruct((frames, phases, 1, cells), f32),
        in_specs=[pl.BlockSpec(memory_space=pl.ANY)] * 3,
        out_specs=pl.BlockSpec(memory_space=pltpu.VMEM),
        scratch_shapes=[
            pltpu.VMEM((KSIDE, KSIDE, phases, phases), bf16),
            pltpu.VMEM((frames, phases, 1, cells), f32),
            pltpu.VMEM((phases, frames, cells), f32),
            pltpu.VMEM((frames, 3 * cells, phases), bf16),
            pltpu.VMEM((frames, 3 * cells, phases), bf16),
            pltpu.VMEM((rows, phases), f32),
            pltpu.VMEM((rows, phases), f32),
            pltpu.VMEM((KSIDE, rows, phases), f32),
            pltpu.VMEM((16, phases), f32),
            pltpu.VMEM((rows, phases), bf16),
            pltpu.VMEM((plane, block, phases), bf16),
            pltpu.VMEM((block, phases), bf16),
            pltpu.VMEM((lines, block, phases), bf16),
            dma((KSIDE,)), dma((2,)), dma((2,)), dma((2,)),
            dma, dma, dma, dma, dma((3,)), dma((3,)),
            pltpu.SemaphoreType.REGULAR((4,)),
        ],
        compiler_params=pltpu.CompilerParams(
            collective_id=0, has_side_effects=True, vmem_limit_bytes=48 << 20),
    )(*(pltpu.with_memory_space_constraint(x, pltpu.HBM) for x in (vol, ker, meas)))
    return out.transpose(0, 2, 1, 3)


def solution(mesh):
    in_specs = (P(None, "depth", None, "tile"), P("depth", None, None, None), P(None, None, "tile"))
    out_specs = P(None, "depth", None, "tile")
    return jax.shard_map(
        functools.partial(local, mesh.shape["depth"], mesh.shape["tile"]),
        mesh=mesh, in_specs=in_specs, out_specs=out_specs, check_vma=False)
```

```python
import functools

import jax
import jax.numpy as jnp
from jax import lax
from jax.experimental import pallas as pl
from jax.experimental.pallas import tpu as pltpu
from jax.sharding import PartitionSpec as P

KSIDE = 9
HALF = 4
COLS = 32
FRAMES = 2
AHEAD = 4
MESH = pl.DeviceIdType.MESH


def partial_sums(src, taps, sign, cells, own, transposed):
    height = cells // COLS
    phases = src.shape[-1]
    sums = [None] * height
    for a in range(KSIDE):
        u = sign * (a - HALF)
        if own:
            low, high = max(0, -u), min(height, height - u)
        else:
            low, high = (max(0, height - u), height) if u > 0 else (0, min(height, -u))
        if low >= high:
            continue
        start = cells + COLS * (low + u)
        count = high - low
        lhs = src[:, start:start + COLS * count, :].reshape(FRAMES * COLS * count, phases)
        dims = (((1,), (1 if transposed else 0,)), ((), ()))
        out = lax.dot_general(lhs, taps[a], dims, preferred_element_type=jnp.float32)
        out = out.reshape(FRAMES, count, COLS, phases)
        for i in range(count):
            piece = out[:, i]
            sums[low + i] = piece if sums[low + i] is None else sums[low + i] + piece
    return jnp.stack(sums, axis=1).reshape(FRAMES * cells, phases)


def step(plane, lines, tiles, vol, ker, meas, out, kbuf, vbuf, mbuf, vx, rx, mt, acc, parts,
         nrm, psend, precv, zsend, zrecv, ksem, lsem, hs, hr, ps, pr, zs, zr, gs, gr, round_sem):
    phases = ker.shape[2]
    cells = vol.shape[-1]
    rows = FRAMES * cells
    block = rows // plane
    d = lax.axis_index("depth")
    t = lax.axis_index("tile")
    z = d // plane
    k = d % plane
    first = t == 0
    last = t == tiles - 1

    load_vol = pltpu.make_async_copy(vol, vbuf, lsem.at[0])
    load_meas = pltpu.make_async_copy(meas, mbuf, lsem.at[1])
    load_vol.start()

    def load_kernel(b):
        return pltpu.make_async_copy(ker.at[:, b], kbuf.at[b], ksem.at[b])

    pair = 1 - 2 * (t % 2)
    far = t - pair
    crossing = (far >= 0) & (far < tiles)
    relayed = plane == 8 and lines == 8

    def tell(sem, depth, tile):
        pl.semaphore_signal(sem, inc=1, device_id=(depth, tile), device_id_type=MESH)

    def along(j):
        return ((z + lines + j) % lines) * plane + k

    def flat(j):
        return z * plane + (k + j) % plane

    across = z * plane + (k + plane // 2) % plane
    barrier = pltpu.get_barrier_semaphore()
    if relayed:
        row = z * plane + (k // 4) * 4
        for j in range(1, 4):
            tell(barrier, row + (k + j) % 4, t)
        tell(barrier, across, t)
        for j in (-2, -1, 1, 2):
            tell(barrier, along(j), t)
        near = 8
    else:
        for j in range(1, plane):
            tell(barrier, flat(j), t)
        for j in range(1, lines):
            tell(barrier, along(j), t)
        near = plane + lines - 2
    tell(barrier, d, t + pair)

    @pl.when(crossing)
    def _():
        tell(barrier, d, far)

    @pl.when(first)
    def _():
        vx[:, 0:cells, :] = jnp.zeros((FRAMES, cells, phases), jnp.bfloat16)
        rx[:, 0:cells, :] = jnp.zeros((FRAMES, cells, phases), jnp.bfloat16)

    @pl.when(last)
    def _():
        vx[:, 2 * cells:, :] = jnp.zeros((FRAMES, cells, phases), jnp.bfloat16)
        rx[:, 2 * cells:, :] = jnp.zeros((FRAMES, cells, phases), jnp.bfloat16)

    for b in range(AHEAD):
        load_kernel(b).start()
    load_vol.wait()
    for f in range(FRAMES):
        vx[f, cells:2 * cells, :] = vbuf[f, :, 0, :].T.astype(jnp.bfloat16)

    pl.semaphore_wait(barrier, near + 1 + jnp.where(crossing, 1, 0))

    own = vx.at[:, pl.ds(cells, cells), :]
    to_next = pltpu.make_async_remote_copy(
        own, vx.at[:, pl.ds(0, cells), :], hs.at[0], hr.at[0], device_id=(d, t + 1), device_id_type=MESH)
    to_prev = pltpu.make_async_remote_copy(
        own, vx.at[:, pl.ds(2 * cells, cells), :], hs.at[1], hr.at[1], device_id=(d, t - 1), device_id_type=MESH)

    @pl.when(t < tiles - 1)
    def _():
        to_next.start()

    @pl.when(t > 0)
    def _():
        to_prev.start()

    if relayed:
        tell(round_sem.at[0], along(-2), t)
        tell(round_sem.at[1], along(2), t)
        tell(round_sem.at[2], across, t)

    load_meas.start()

    @pl.loop(0, KSIDE)
    def _(b):
        load_kernel(b).wait()

        @pl.when(b < KSIDE - AHEAD)
        def _():
            load_kernel(b + AHEAD).start()

        parts[b] = partial_sums(vx, kbuf.at[b], 1, cells, True, True)

    if relayed:
        pl.semaphore_wait(round_sem.at[2], 1)
    @pl.when(crossing)
    def _():
        tell(round_sem.at[3], d, far)

    @pl.when(t > 0)
    def _():
        to_next.wait_recv()

    @pl.when(t < tiles - 1)
    def _():
        to_prev.wait_recv()

    column = lax.broadcasted_iota(jnp.int32, (rows, phases), 0) % COLS

    def shifted(total, shift):
        if shift == 0:
            return total
        moved = column - shift
        return jnp.where((moved >= 0) & (moved < COLS), pltpu.roll(total, shift % rows, 0), 0.0)

    for b in range(KSIDE):
        total = parts[b] + partial_sums(vx, kbuf.at[b], 1, cells, False, True)
        add = shifted(total, HALF - b)
        acc[...] = add if b == 0 else acc[...] + add

    if relayed:
        pl.semaphore_wait(round_sem.at[0], 1)
        pl.semaphore_wait(round_sem.at[1], 1)

    @pl.when(crossing)
    def _():
        pl.semaphore_wait(round_sem.at[3], 1)

    psend[...] = acc[...].astype(jnp.bfloat16)
    for j in range(1, plane):
        peer = (k + j) % plane
        pltpu.make_async_remote_copy(
            psend.at[pl.ds(pl.multiple_of(peer * block, block), block), :], precv.at[j], ps, pr,
            device_id=(z * plane + peer, t), device_id_type=MESH).start()

    def landed(ref, sem):
        pltpu.make_async_copy(ref, ref, sem).wait()

    others = pl.ds(1, plane - 1)
    load_meas.wait()
    for f in range(FRAMES):
        mt[f * cells:(f + 1) * cells, :] = mbuf[:, f, :].T

    mine = pl.ds(pl.multiple_of(k * block, block), block)
    part = acc[mine, :]
    landed(precv.at[others], pr)
    for j in range(1, plane):
        part += precv[j].astype(jnp.float32)

    zsend[...] = part.astype(jnp.bfloat16)
    for j in range(1, lines):
        pltpu.make_async_remote_copy(
            zsend, zrecv.at[j], zs, zr, device_id=(along(j), t), device_id_type=MESH).start()
    landed(zrecv.at[pl.ds(1, lines - 1)], zr)
    for j in range(1, lines):
        part += zrecv[j].astype(jnp.float32)

    ratio = (mt[mine, :] / part).astype(jnp.bfloat16)
    fk = (k * block) // cells
    rk = (k * block) % cells

    def place(base, who):
        f = (who * block) // cells
        r = (who * block) % cells
        return rx.at[f, pl.ds(pl.multiple_of(base + r, block), block), :]

    rx[fk, pl.ds(pl.multiple_of(cells + rk, block), block), :] = ratio

    for j in range(1, plane):
        pltpu.make_async_remote_copy(
            place(cells, k), place(cells, k), gs.at[0], gr.at[0],
            device_id=(flat(j), t), device_id_type=MESH).start()

    @pl.when(crossing)
    def _():
        for j in range(plane):
            pltpu.make_async_remote_copy(
                place(cells, k), place((1 + pair) * cells, k), gs.at[1], gr.at[1],
                device_id=(flat(j), far), device_id_type=MESH).start()

    ones = jnp.ones((16, phases), jnp.bfloat16)
    nrm[...] = jnp.zeros_like(nrm)

    @pl.loop(0, KSIDE)
    def _(b):
        total = None
        for a in range(KSIDE):
            term = jnp.dot(ones, kbuf[b, a], preferred_element_type=jnp.float32)
            total = term if total is None else total + term
        nrm[...] += total

    relay = pltpu.make_async_remote_copy(
        rx.at[:, pl.ds(cells, cells), :], rx.at[:, pl.ds(pl.multiple_of((1 - pair) * cells, cells), cells), :],
        gs.at[2], gr.at[2], device_id=(d, t + pair), device_id_type=MESH)
    landed(precv.at[others], gr.at[0])
    relay.start()

    @pl.loop(0, KSIDE, unroll=3)
    def _(b):
        parts[b] = partial_sums(rx, kbuf.at[b], -1, cells, True, False)

    relay.wait_recv()

    @pl.when(crossing)
    def _():
        landed(rx.at[:, pl.ds(0, cells), :], gr.at[1])

    for b in range(KSIDE):
        total = parts[b] + partial_sums(rx, kbuf.at[b], -1, cells, False, False)
        add = shifted(total, b - HALF)
        acc[...] = add if b == 0 else acc[...] + add

    norm = nrm[0:1, :]
    for f in range(FRAMES):
        scaled = acc[f * cells:(f + 1) * cells, :] / norm
        out[f, :, 0, :] = vbuf[f, :, 0, :] * scaled.T

    landed(precv.at[others], ps)
    landed(zrecv.at[pl.ds(1, lines - 1)], zs)
    landed(precv.at[others], gs.at[0])
    relay.wait_send()

    @pl.when(crossing)
    def _():
        landed(rx.at[:, pl.ds(0, cells), :], gs.at[1])

    @pl.when(t < tiles - 1)
    def _():
        to_next.wait_send()

    @pl.when(t > 0)
    def _():
        to_prev.wait_send()


def local(depths, tiles, volume, kernel, measured):
    frames, _, phases, cells = volume.shape
    plane = 8 if depths % 8 == 0 else 2
    lines = depths // plane
    rows = frames * cells
    block = rows // plane
    vol = volume.transpose(0, 2, 1, 3)
    ker = kernel.transpose(0, 2, 1, 3).reshape(KSIDE, KSIDE, phases, phases)
    meas = measured.transpose(1, 0, 2)
    bf16, f32 = jnp.bfloat16, jnp.float32
    dma = pltpu.SemaphoreType.DMA
    out = pl.pallas_call(
        functools.partial(step, plane, lines, tiles),
        out_shape=jax.ShapeDtypeStruct((frames, phases, 1, cells), f32),
        in_specs=[pl.BlockSpec(memory_space=pl.ANY)] * 3,
        out_specs=pl.BlockSpec(memory_space=pltpu.VMEM),
        scratch_shapes=[
            pltpu.VMEM((KSIDE, KSIDE, phases, phases), bf16),
            pltpu.VMEM((frames, phases, 1, cells), f32),
            pltpu.VMEM((phases, frames, cells), f32),
            pltpu.VMEM((frames, 3 * cells, phases), bf16),
            pltpu.VMEM((frames, 3 * cells, phases), bf16),
            pltpu.VMEM((rows, phases), f32),
            pltpu.VMEM((rows, phases), f32),
            pltpu.VMEM((KSIDE, rows, phases), f32),
            pltpu.VMEM((16, phases), f32),
            pltpu.VMEM((rows, phases), bf16),
            pltpu.VMEM((plane, block, phases), bf16),
            pltpu.VMEM((block, phases), bf16),
            pltpu.VMEM((lines, block, phases), bf16),
            dma((KSIDE,)), dma((2,)), dma((2,)), dma((2,)),
            dma, dma, dma, dma, dma((3,)), dma((3,)),
            pltpu.SemaphoreType.REGULAR((4,)),
        ],
        compiler_params=pltpu.CompilerParams(
            collective_id=0, has_side_effects=True, vmem_limit_bytes=48 << 20),
    )(*(pltpu.with_memory_space_constraint(x, pltpu.HBM) for x in (vol, ker, meas)))
    return out.transpose(0, 2, 1, 3)


def solution(mesh):
    in_specs = (P(None, "depth", None, "tile"), P("depth", None, None, None), P(None, None, "tile"))
    out_specs = P(None, "depth", None, "tile")
    return jax.shard_map(
        functools.partial(local, mesh.shape["depth"], mesh.shape["tile"]),
        mesh=mesh, in_specs=in_specs, out_specs=out_specs, check_vma=False)
```

```python
import functools

import jax
import jax.numpy as jnp
from jax import lax
from jax.experimental import pallas as pl
from jax.experimental.pallas import tpu as pltpu
from jax.sharding import PartitionSpec as P

KSIDE = 9
HALF = 4
COLS = 32
FRAMES = 2
AHEAD = 4
MESH = pl.DeviceIdType.MESH


def partial_sums(src, taps, sign, cells, own, transposed):
    height = cells // COLS
    phases = src.shape[-1]
    sums = [None] * height
    for a in range(KSIDE):
        u = sign * (a - HALF)
        if own:
            low, high = max(0, -u), min(height, height - u)
        else:
            low, high = (max(0, height - u), height) if u > 0 else (0, min(height, -u))
        if low >= high:
            continue
        start = cells + COLS * (low + u)
        count = high - low
        lhs = src[:, start:start + COLS * count, :].reshape(FRAMES * COLS * count, phases)
        dims = (((1,), (1 if transposed else 0,)), ((), ()))
        out = lax.dot_general(lhs, taps[a], dims, preferred_element_type=jnp.float32)
        out = out.reshape(FRAMES, count, COLS, phases)
        for i in range(count):
            piece = out[:, i]
            sums[low + i] = piece if sums[low + i] is None else sums[low + i] + piece
    return jnp.stack(sums, axis=1).reshape(FRAMES * cells, phases)


def step(plane, lines, tiles, vol, ker, meas, out, kbuf, vbuf, mbuf, vx, rx, mt, acc, parts,
         nrm, psend, precv, zsend, zrecv, ksem, lsem, hs, hr, ps, pr, zs, zr, gs, gr, round_sem):
    phases = ker.shape[2]
    cells = vol.shape[-1]
    rows = FRAMES * cells
    block = rows // plane
    d = lax.axis_index("depth")
    t = lax.axis_index("tile")
    z = d // plane
    k = d % plane
    first = t == 0
    last = t == tiles - 1

    load_vol = pltpu.make_async_copy(vol, vbuf, lsem.at[0])
    load_meas = pltpu.make_async_copy(meas, mbuf, lsem.at[1])
    load_vol.start()

    def load_kernel(b):
        return pltpu.make_async_copy(ker.at[:, b], kbuf.at[b], ksem.at[b])

    pair = 1 - 2 * (t % 2)
    far = t - pair
    crossing = (far >= 0) & (far < tiles)
    relayed = plane == 8 and lines == 8

    def tell(sem, depth, tile):
        pl.semaphore_signal(sem, inc=1, device_id=(depth, tile), device_id_type=MESH)

    def along(j):
        return ((z + lines + j) % lines) * plane + k

    def flat(j):
        return z * plane + (k + j) % plane

    across = z * plane + (k + plane // 2) % plane
    barrier = pltpu.get_barrier_semaphore()
    tell(barrier, d, t + pair)
    for b in range(AHEAD):
        load_kernel(b).start()
    if relayed:
        row = z * plane + (k // 4) * 4
        for j in range(1, 4):
            tell(barrier, row + (k + j) % 4, t)
        tell(barrier, across, t)
        for j in (-2, -1, 1, 2):
            tell(barrier, along(j), t)
        near = 8
    else:
        for j in range(1, plane):
            tell(barrier, flat(j), t)
        for j in range(1, lines):
            tell(barrier, along(j), t)
        near = plane + lines - 2

    @pl.when(crossing)
    def _():
        tell(barrier, d, far)

    @pl.when(first)
    def _():
        vx[:, 0:cells, :] = jnp.zeros((FRAMES, cells, phases), jnp.bfloat16)
        rx[:, 0:cells, :] = jnp.zeros((FRAMES, cells, phases), jnp.bfloat16)

    @pl.when(last)
    def _():
        vx[:, 2 * cells:, :] = jnp.zeros((FRAMES, cells, phases), jnp.bfloat16)
        rx[:, 2 * cells:, :] = jnp.zeros((FRAMES, cells, phases), jnp.bfloat16)

    load_vol.wait()
    for f in range(FRAMES):
        vx[f, cells:2 * cells, :] = vbuf[f, :, 0, :].T.astype(jnp.bfloat16)

    pl.semaphore_wait(barrier, near + 1 + jnp.where(crossing, 1, 0))

    own = vx.at[:, pl.ds(cells, cells), :]
    to_next = pltpu.make_async_remote_copy(
        own, vx.at[:, pl.ds(0, cells), :], hs.at[0], hr.at[0], device_id=(d, t + 1), device_id_type=MESH)
    to_prev = pltpu.make_async_remote_copy(
        own, vx.at[:, pl.ds(2 * cells, cells), :], hs.at[1], hr.at[1], device_id=(d, t - 1), device_id_type=MESH)

    @pl.when(t < tiles - 1)
    def _():
        to_next.start()

    @pl.when(t > 0)
    def _():
        to_prev.start()

    if relayed:
        tell(round_sem.at[0], along(-2), t)
        tell(round_sem.at[1], along(2), t)
        tell(round_sem.at[2], across, t)

    load_meas.start()

    @pl.loop(0, KSIDE)
    def _(b):
        load_kernel(b).wait()

        @pl.when(b < KSIDE - AHEAD)
        def _():
            load_kernel(b + AHEAD).start()

        parts[b] = partial_sums(vx, kbuf.at[b], 1, cells, True, True)

    if relayed:
        pl.semaphore_wait(round_sem.at[2], 1)
    @pl.when(crossing)
    def _():
        tell(round_sem.at[3], d, far)

    @pl.when(t > 0)
    def _():
        to_next.wait_recv()

    @pl.when(t < tiles - 1)
    def _():
        to_prev.wait_recv()

    column = lax.broadcasted_iota(jnp.int32, (rows, phases), 0) % COLS

    def shifted(total, shift):
        if shift == 0:
            return total
        moved = column - shift
        return jnp.where((moved >= 0) & (moved < COLS), pltpu.roll(total, shift % rows, 0), 0.0)

    for b in range(KSIDE):
        total = parts[b] + partial_sums(vx, kbuf.at[b], 1, cells, False, True)
        add = shifted(total, HALF - b)
        acc[...] = add if b == 0 else acc[...] + add

    if relayed:
        pl.semaphore_wait(round_sem.at[0], 1)
        pl.semaphore_wait(round_sem.at[1], 1)

    @pl.when(crossing)
    def _():
        pl.semaphore_wait(round_sem.at[3], 1)

    psend[...] = acc[...].astype(jnp.bfloat16)
    for j in range(1, plane):
        peer = (k + j) % plane
        pltpu.make_async_remote_copy(
            psend.at[pl.ds(pl.multiple_of(peer * block, block), block), :], precv.at[j], ps, pr,
            device_id=(z * plane + peer, t), device_id_type=MESH).start()

    def landed(ref, sem):
        pltpu.make_async_copy(ref, ref, sem).wait()

    others = pl.ds(1, plane - 1)
    load_meas.wait()
    for f in range(FRAMES):
        mt[f * cells:(f + 1) * cells, :] = mbuf[:, f, :].T

    mine = pl.ds(pl.multiple_of(k * block, block), block)
    part = acc[mine, :]
    landed(precv.at[others], pr)
    for j in range(1, plane):
        part += precv[j].astype(jnp.float32)

    zsend[...] = part.astype(jnp.bfloat16)
    for j in sorted(range(1, lines), key=lambda j: -min(j, lines - j)):
        pltpu.make_async_remote_copy(
            zsend, zrecv.at[j], zs, zr, device_id=(along(j), t), device_id_type=MESH).start()
    landed(zrecv.at[pl.ds(1, lines - 1)], zr)
    for j in range(1, lines):
        part += zrecv[j].astype(jnp.float32)

    ratio = (mt[mine, :] / part).astype(jnp.bfloat16)
    fk = (k * block) // cells
    rk = (k * block) % cells

    def place(base, who):
        f = (who * block) // cells
        r = (who * block) % cells
        return rx.at[f, pl.ds(pl.multiple_of(base + r, block), block), :]

    rx[fk, pl.ds(pl.multiple_of(cells + rk, block), block), :] = ratio

    @pl.when(crossing)
    def _():
        for j in range(plane):
            pltpu.make_async_remote_copy(
                place(cells, k), place((1 + pair) * cells, k), gs.at[1], gr.at[1],
                device_id=(flat(j), far), device_id_type=MESH).start()

    for j in range(1, plane):
        pltpu.make_async_remote_copy(
            place(cells, k), place(cells, k), gs.at[0], gr.at[0],
            device_id=(flat(j), t), device_id_type=MESH).start()

    ones = jnp.ones((16, phases), jnp.bfloat16)
    nrm[...] = jnp.zeros_like(nrm)

    @pl.loop(0, KSIDE)
    def _(b):
        total = None
        for a in range(KSIDE):
            term = jnp.dot(ones, kbuf[b, a], preferred_element_type=jnp.float32)
            total = term if total is None else total + term
        nrm[...] += total

    relay = pltpu.make_async_remote_copy(
        rx.at[:, pl.ds(cells, cells), :], rx.at[:, pl.ds(pl.multiple_of((1 - pair) * cells, cells), cells), :],
        gs.at[2], gr.at[2], device_id=(d, t + pair), device_id_type=MESH)
    landed(precv.at[others], gr.at[0])
    relay.start()

    @pl.loop(0, KSIDE, unroll=3)
    def _(b):
        parts[b] = partial_sums(rx, kbuf.at[b], -1, cells, True, False)

    relay.wait_recv()

    @pl.when(crossing)
    def _():
        landed(rx.at[:, pl.ds(0, cells), :], gr.at[1])

    for b in range(KSIDE):
        total = parts[b] + partial_sums(rx, kbuf.at[b], -1, cells, False, False)
        add = shifted(total, b - HALF)
        acc[...] = add if b == 0 else acc[...] + add

    norm = nrm[0:1, :]
    for f in range(FRAMES):
        scaled = acc[f * cells:(f + 1) * cells, :] / norm
        out[f, :, 0, :] = vbuf[f, :, 0, :] * scaled.T

    landed(precv.at[others], ps)
    landed(zrecv.at[pl.ds(1, lines - 1)], zs)
    landed(precv.at[others], gs.at[0])
    relay.wait_send()

    @pl.when(crossing)
    def _():
        landed(rx.at[:, pl.ds(0, cells), :], gs.at[1])

    @pl.when(t < tiles - 1)
    def _():
        to_next.wait_send()

    @pl.when(t > 0)
    def _():
        to_prev.wait_send()


def local(depths, tiles, volume, kernel, measured):
    frames, _, phases, cells = volume.shape
    plane = 8 if depths % 8 == 0 else 2
    lines = depths // plane
    rows = frames * cells
    block = rows // plane
    vol = volume.transpose(0, 2, 1, 3)
    ker = kernel.transpose(0, 2, 1, 3).reshape(KSIDE, KSIDE, phases, phases)
    meas = measured.transpose(1, 0, 2)
    bf16, f32 = jnp.bfloat16, jnp.float32
    dma = pltpu.SemaphoreType.DMA
    out = pl.pallas_call(
        functools.partial(step, plane, lines, tiles),
        out_shape=jax.ShapeDtypeStruct((frames, phases, 1, cells), f32),
        in_specs=[pl.BlockSpec(memory_space=pl.ANY)] * 3,
        out_specs=pl.BlockSpec(memory_space=pltpu.VMEM),
        scratch_shapes=[
            pltpu.VMEM((KSIDE, KSIDE, phases, phases), bf16),
            pltpu.VMEM((frames, phases, 1, cells), f32),
            pltpu.VMEM((phases, frames, cells), f32),
            pltpu.VMEM((frames, 3 * cells, phases), bf16),
            pltpu.VMEM((frames, 3 * cells, phases), bf16),
            pltpu.VMEM((rows, phases), f32),
            pltpu.VMEM((rows, phases), f32),
            pltpu.VMEM((KSIDE, rows, phases), f32),
            pltpu.VMEM((16, phases), f32),
            pltpu.VMEM((rows, phases), bf16),
            pltpu.VMEM((plane, block, phases), bf16),
            pltpu.VMEM((block, phases), bf16),
            pltpu.VMEM((lines, block, phases), bf16),
            dma((KSIDE,)), dma((2,)), dma((2,)), dma((2,)),
            dma, dma, dma, dma, dma((3,)), dma((3,)),
            pltpu.SemaphoreType.REGULAR((4,)),
        ],
        compiler_params=pltpu.CompilerParams(
            collective_id=0, has_side_effects=True, vmem_limit_bytes=48 << 20),
    )(*(pltpu.with_memory_space_constraint(x, pltpu.HBM) for x in (vol, ker, meas)))
    return out.transpose(0, 2, 1, 3)


def solution(mesh):
    in_specs = (P(None, "depth", None, "tile"), P("depth", None, None, None), P(None, None, "tile"))
    out_specs = P(None, "depth", None, "tile")
    return jax.shard_map(
        functools.partial(local, mesh.shape["depth"], mesh.shape["tile"]),
        mesh=mesh, in_specs=in_specs, out_specs=out_specs, check_vma=False)
```

```python
import functools

import jax
import jax.numpy as jnp
from jax import lax
from jax.experimental import pallas as pl
from jax.experimental.pallas import tpu as pltpu
from jax.sharding import PartitionSpec as P

KSIDE = 9
HALF = 4
COLS = 32
FRAMES = 2
AHEAD = 4
MESH = pl.DeviceIdType.MESH


def partial_sums(src, taps, sign, cells, own, transposed):
    height = cells // COLS
    phases = src.shape[-1]
    sums = [None] * height
    for a in range(KSIDE):
        u = sign * (a - HALF)
        if own:
            low, high = max(0, -u), min(height, height - u)
        else:
            low, high = (max(0, height - u), height) if u > 0 else (0, min(height, -u))
        if low >= high:
            continue
        start = cells + COLS * (low + u)
        count = high - low
        lhs = src[:, start:start + COLS * count, :].reshape(FRAMES * COLS * count, phases)
        dims = (((1,), (1 if transposed else 0,)), ((), ()))
        out = lax.dot_general(lhs, taps[a], dims, preferred_element_type=jnp.float32)
        out = out.reshape(FRAMES, count, COLS, phases)
        for i in range(count):
            piece = out[:, i]
            sums[low + i] = piece if sums[low + i] is None else sums[low + i] + piece
    return jnp.stack(sums, axis=1).reshape(FRAMES * cells, phases)


def step(plane, lines, tiles, vol, ker, meas, out, kbuf, vbuf, mbuf, vx, rx, mt, acc, parts,
         nrm, psend, precv, zsend, zrecv, ksem, lsem, hs, hr, ps, pr, zs, zr, gs, gr, round_sem):
    phases = ker.shape[2]
    cells = vol.shape[-1]
    rows = FRAMES * cells
    block = rows // plane
    d = lax.axis_index("depth")
    t = lax.axis_index("tile")
    z = d // plane
    k = d % plane
    first = t == 0
    last = t == tiles - 1

    load_vol = pltpu.make_async_copy(vol, vbuf, lsem.at[0])
    load_meas = pltpu.make_async_copy(meas, mbuf, lsem.at[1])
    load_vol.start()

    def load_kernel(b):
        return pltpu.make_async_copy(ker.at[:, b], kbuf.at[b], ksem.at[b])

    pair = 1 - 2 * (t % 2)
    far = t - pair
    crossing = (far >= 0) & (far < tiles)
    relayed = plane == 8 and lines == 8

    def tell(sem, depth, tile):
        pl.semaphore_signal(sem, inc=1, device_id=(depth, tile), device_id_type=MESH)

    def along(j):
        return ((z + lines + j) % lines) * plane + k

    def flat(j):
        return z * plane + (k + j) % plane

    across = z * plane + (k + plane // 2) % plane
    barrier = pltpu.get_barrier_semaphore()
    tell(barrier, d, t + pair)
    for b in range(AHEAD):
        load_kernel(b).start()
    if relayed:
        row = z * plane + (k // 4) * 4
        for j in range(1, 4):
            tell(barrier, row + (k + j) % 4, t)
        tell(barrier, across, t)
        for j in (-2, -1, 1, 2):
            tell(barrier, along(j), t)
        near = 8
    else:
        for j in range(1, plane):
            tell(barrier, flat(j), t)
        for j in range(1, lines):
            tell(barrier, along(j), t)
        near = plane + lines - 2

    @pl.when(crossing)
    def _():
        tell(barrier, d, far)

    @pl.when(first)
    def _():
        vx[:, 0:cells, :] = jnp.zeros((FRAMES, cells, phases), jnp.bfloat16)
        rx[:, 0:cells, :] = jnp.zeros((FRAMES, cells, phases), jnp.bfloat16)

    @pl.when(last)
    def _():
        vx[:, 2 * cells:, :] = jnp.zeros((FRAMES, cells, phases), jnp.bfloat16)
        rx[:, 2 * cells:, :] = jnp.zeros((FRAMES, cells, phases), jnp.bfloat16)

    load_vol.wait()
    for f in range(FRAMES):
        vx[f, cells:2 * cells, :] = vbuf[f, :, 0, :].T.astype(jnp.bfloat16)

    pl.semaphore_wait(barrier, near + 1 + jnp.where(crossing, 1, 0))

    own = vx.at[:, pl.ds(cells, cells), :]
    to_next = pltpu.make_async_remote_copy(
        own, vx.at[:, pl.ds(0, cells), :], hs.at[0], hr.at[0], device_id=(d, t + 1), device_id_type=MESH)
    to_prev = pltpu.make_async_remote_copy(
        own, vx.at[:, pl.ds(2 * cells, cells), :], hs.at[1], hr.at[1], device_id=(d, t - 1), device_id_type=MESH)

    @pl.when(t < tiles - 1)
    def _():
        to_next.start()

    @pl.when(t > 0)
    def _():
        to_prev.start()

    if relayed:
        tell(round_sem.at[0], along(-2), t)
        tell(round_sem.at[1], along(2), t)
        tell(round_sem.at[2], across, t)

    load_meas.start()

    @pl.loop(0, KSIDE)
    def _(b):
        load_kernel(b).wait()

        @pl.when(b < KSIDE - AHEAD)
        def _():
            load_kernel(b + AHEAD).start()

        parts[b] = partial_sums(vx, kbuf.at[b], 1, cells, True, True)

    if relayed:
        pl.semaphore_wait(round_sem.at[2], 1)
    @pl.when(crossing)
    def _():
        tell(round_sem.at[3], d, far)

    @pl.when(t > 0)
    def _():
        to_next.wait_recv()

    @pl.when(t < tiles - 1)
    def _():
        to_prev.wait_recv()

    column = lax.broadcasted_iota(jnp.int32, (rows, phases), 0) % COLS

    def shifted(total, shift):
        if shift == 0:
            return total
        moved = column - shift
        return jnp.where((moved >= 0) & (moved < COLS), pltpu.roll(total, shift % rows, 0), 0.0)

    for b in range(KSIDE):
        total = parts[b] + partial_sums(vx, kbuf.at[b], 1, cells, False, True)
        add = shifted(total, HALF - b)
        acc[...] = add if b == 0 else acc[...] + add

    if relayed:
        pl.semaphore_wait(round_sem.at[0], 1)
        pl.semaphore_wait(round_sem.at[1], 1)

    @pl.when(crossing)
    def _():
        pl.semaphore_wait(round_sem.at[3], 1)

    psend[...] = acc[...].astype(jnp.bfloat16)
    for j in sorted(range(1, plane), key=lambda j: abs(2 - j % 4)):
        peer = (k + j) % plane
        pltpu.make_async_remote_copy(
            psend.at[pl.ds(pl.multiple_of(peer * block, block), block), :], precv.at[j], ps, pr,
            device_id=(z * plane + peer, t), device_id_type=MESH).start()

    def landed(ref, sem):
        pltpu.make_async_copy(ref, ref, sem).wait()

    others = pl.ds(1, plane - 1)
    load_meas.wait()
    for f in range(FRAMES):
        mt[f * cells:(f + 1) * cells, :] = mbuf[:, f, :].T

    mine = pl.ds(pl.multiple_of(k * block, block), block)
    part = acc[mine, :]
    landed(precv.at[others], pr)
    for j in range(1, plane):
        part += precv[j].astype(jnp.float32)

    zsend[...] = part.astype(jnp.bfloat16)
    for j in sorted(range(1, lines), key=lambda j: -min(j, lines - j)):
        pltpu.make_async_remote_copy(
            zsend, zrecv.at[j], zs, zr, device_id=(along(j), t), device_id_type=MESH).start()
    landed(zrecv.at[pl.ds(1, lines - 1)], zr)
    for j in range(1, lines):
        part += zrecv[j].astype(jnp.float32)

    ratio = (mt[mine, :] / part).astype(jnp.bfloat16)
    fk = (k * block) // cells
    rk = (k * block) % cells

    def place(base, who):
        f = (who * block) // cells
        r = (who * block) % cells
        return rx.at[f, pl.ds(pl.multiple_of(base + r, block), block), :]

    rx[fk, pl.ds(pl.multiple_of(cells + rk, block), block), :] = ratio

    @pl.when(crossing)
    def _():
        for j in sorted(range(plane), key=lambda j: abs(2 - j % 4)):
            pltpu.make_async_remote_copy(
                place(cells, k), place((1 + pair) * cells, k), gs.at[1], gr.at[1],
                device_id=(flat(j), far), device_id_type=MESH).start()

    for j in sorted(range(1, plane), key=lambda j: abs(2 - j % 4)):
        pltpu.make_async_remote_copy(
            place(cells, k), place(cells, k), gs.at[0], gr.at[0],
            device_id=(flat(j), t), device_id_type=MESH).start()

    ones = jnp.ones((16, phases), jnp.bfloat16)
    nrm[...] = jnp.zeros_like(nrm)

    @pl.loop(0, KSIDE)
    def _(b):
        total = None
        for a in range(KSIDE):
            term = jnp.dot(ones, kbuf[b, a], preferred_element_type=jnp.float32)
            total = term if total is None else total + term
        nrm[...] += total

    relay = pltpu.make_async_remote_copy(
        rx.at[:, pl.ds(cells, cells), :], rx.at[:, pl.ds(pl.multiple_of((1 - pair) * cells, cells), cells), :],
        gs.at[2], gr.at[2], device_id=(d, t + pair), device_id_type=MESH)
    landed(precv.at[others], gr.at[0])
    relay.start()

    @pl.loop(0, KSIDE, unroll=3)
    def _(b):
        parts[b] = partial_sums(rx, kbuf.at[b], -1, cells, True, False)

    relay.wait_recv()

    @pl.when(crossing)
    def _():
        landed(rx.at[:, pl.ds(0, cells), :], gr.at[1])

    for b in range(KSIDE):
        total = parts[b] + partial_sums(rx, kbuf.at[b], -1, cells, False, False)
        add = shifted(total, b - HALF)
        acc[...] = add if b == 0 else acc[...] + add

    norm = nrm[0:1, :]
    for f in range(FRAMES):
        scaled = acc[f * cells:(f + 1) * cells, :] / norm
        out[f, :, 0, :] = vbuf[f, :, 0, :] * scaled.T

    landed(precv.at[others], ps)
    landed(zrecv.at[pl.ds(1, lines - 1)], zs)
    landed(precv.at[others], gs.at[0])
    relay.wait_send()

    @pl.when(crossing)
    def _():
        landed(rx.at[:, pl.ds(0, cells), :], gs.at[1])

    @pl.when(t < tiles - 1)
    def _():
        to_next.wait_send()

    @pl.when(t > 0)
    def _():
        to_prev.wait_send()


def local(depths, tiles, volume, kernel, measured):
    frames, _, phases, cells = volume.shape
    plane = 8 if depths % 8 == 0 else 2
    lines = depths // plane
    rows = frames * cells
    block = rows // plane
    vol = volume.transpose(0, 2, 1, 3)
    ker = kernel.transpose(0, 2, 1, 3).reshape(KSIDE, KSIDE, phases, phases)
    meas = measured.transpose(1, 0, 2)
    bf16, f32 = jnp.bfloat16, jnp.float32
    dma = pltpu.SemaphoreType.DMA
    out = pl.pallas_call(
        functools.partial(step, plane, lines, tiles),
        out_shape=jax.ShapeDtypeStruct((frames, phases, 1, cells), f32),
        in_specs=[pl.BlockSpec(memory_space=pl.ANY)] * 3,
        out_specs=pl.BlockSpec(memory_space=pltpu.VMEM),
        scratch_shapes=[
            pltpu.VMEM((KSIDE, KSIDE, phases, phases), bf16),
            pltpu.VMEM((frames, phases, 1, cells), f32),
            pltpu.VMEM((phases, frames, cells), f32),
            pltpu.VMEM((frames, 3 * cells, phases), bf16),
            pltpu.VMEM((frames, 3 * cells, phases), bf16),
            pltpu.VMEM((rows, phases), f32),
            pltpu.VMEM((rows, phases), f32),
            pltpu.VMEM((KSIDE, rows, phases), f32),
            pltpu.VMEM((16, phases), f32),
            pltpu.VMEM((rows, phases), bf16),
            pltpu.VMEM((plane, block, phases), bf16),
            pltpu.VMEM((block, phases), bf16),
            pltpu.VMEM((lines, block, phases), bf16),
            dma((KSIDE,)), dma((2,)), dma((2,)), dma((2,)),
            dma, dma, dma, dma, dma((3,)), dma((3,)),
            pltpu.SemaphoreType.REGULAR((4,)),
        ],
        compiler_params=pltpu.CompilerParams(
            collective_id=0, has_side_effects=True, vmem_limit_bytes=48 << 20),
    )(*(pltpu.with_memory_space_constraint(x, pltpu.HBM) for x in (vol, ker, meas)))
    return out.transpose(0, 2, 1, 3)


def solution(mesh):
    in_specs = (P(None, "depth", None, "tile"), P("depth", None, None, None), P(None, None, "tile"))
    out_specs = P(None, "depth", None, "tile")
    return jax.shard_map(
        functools.partial(local, mesh.shape["depth"], mesh.shape["tile"]),
        mesh=mesh, in_specs=in_specs, out_specs=out_specs, check_vma=False)
```
